32 devices in a mesh: parts: 2 (over y), tm: 4 (over z), rows: 2 (over x), cols: 2 (over core).
Axes of the slice: x: 2, y: 2, z: 4, core: 2. Of those that a mesh axis runs over, the one named last changes fastest.
Arguments:
- frames: bfloat16 [256, 256, 512], P(('parts', 'tm'), 'rows', 'cols'), parts along dimension 0, may hold values from -6 to 6
- transfer: bfloat16 [256, 128, 128], P(('parts', 'tm')), parts along dimension 0, may hold values from 0.099609375 to 1
- cutoff: int32 [128, 128], replicated, may hold values from 0 to 64
Outputs:
- restored: float32 [256, 256, 512], P(('parts', 'tm'), 'rows', 'cols'), parts along dimension 0
The draws below stay inside these ranges and needn't reach their ends.
There are 2 independent parts, one for each index of `parts`. The reference program is written for one: setup_inputs(seed, part) draws one part's arguments, and reference() takes and returns one part's arrays. A program takes and returns all parts, laid end to end along the dimension named above; an argument that names none is the same for every part. Nothing has to cross between parts.
Inputs may be any that keep to these rules, and one draw needn't show every extreme that they name: cutoff[u, v] is the largest value of min(w, 128 - w) kept at wavenumber (u, v).
All inputs are finite; a program needn't handle non-finite values.
Results may differ from the reference program's by a relative error of at most 0.0003.
Values may be sent and summed in bfloat16 or wider, within the bound.
No kernel may reach another device: no remote copies, remote signals or barrier semaphores. Data moves between devices by JAX's collectives and lax.ppermute only.
A program may use at most 128 MiB of HBM per device.

```python
import math
import jax
import jax.numpy as jnp
from jax import lax

TIME = 128
SUBF = 128
NY = 256
NX = 512


def touch_ends(drawn, own_key, low, high):
    place = [jax.random.randint(jax.random.fold_in(own_key, axis), (), 0, length) for axis, length in enumerate(drawn.shape)]
    widest = drawn.shape.index(max(drawn.shape))
    next_to = place[:widest] + [(place[widest] + 1) % drawn.shape[widest]] + place[widest + 1:]
    return drawn.at[tuple(place)].set(low).at[tuple(next_to)].set(high)


def level_of(rng, shape, shards, low, high):
    def one(position, shards_of):
        draws = jax.random.uniform(jax.random.fold_in(jax.random.fold_in(rng, 6), position), (shards_of,), jnp.float32, low / len(shards), high / len(shards))
        return jnp.repeat(jnp.exp(draws), shape[position] // shards_of).reshape((-1,) + (1,) * (len(shape) - position - 1))

    factor_of = one(*shards[0])
    for cut in shards[1:]:
        factor_of = factor_of * one(*cut)
    return factor_of


def scatter_about(stream_key, shape, deviation, bound, cuts=(), held_as=jnp.bfloat16):
    drawn = jax.random.normal(stream_key, shape, jnp.float32) * deviation
    if len(cuts) > 0:
        drawn = level_of(stream_key, shape, cuts, -0.22, 0.18) * drawn
    return jnp.clip(drawn, min=-bound, max=bound).astype(held_as)


def setup_inputs(seed: int = 0, part: int = 0) -> dict:
    streams_of = jax.random.split(jax.random.key(seed), 4)
    part_splits = jax.random.split(jax.random.fold_in(streams_of[3], part), 4)
    return {
        "frames": scatter_about(part_splits[0], (TIME, NY, NX), 1.0, 6.0, ((0, 4), (1, 2), (2, 2))),
        "transfer": jnp.clip(0.099609375 + 0.9003906 * jax.random.uniform(part_splits[1], (TIME, SUBF, SUBF), jnp.float32) ** level_of(part_splits[1], (TIME, SUBF, SUBF), ((0, 4),), -0.2, 0.2), 0.099609375, 1.0).astype(jnp.bfloat16),
        "cutoff": touch_ends(jax.random.randint(streams_of[2], (SUBF, SUBF), 0, TIME // 2 + 1), jax.random.fold_in(streams_of[2], 1), 0, (TIME // 2 + 1) - 1).astype(jnp.int32),
    }


noise_level = 0.05

def tables(length):
    series = jnp.arange(length, dtype=jnp.int32)
    product = series[:, None] * series[None, :] % length
    angles = product.astype(jnp.float32) * (2.0 * math.pi / length)
    return (jnp.cos(angles), jnp.sin(angles))

def forward_spatial(images, cos_space, sin_space):
    highest = lax.Precision.HIGHEST
    factor = 1.0 / cos_space.shape[0]
    row_real = jnp.einsum('cnab,bv->cnav', images, cos_space, precision=highest)
    row_imag = -jnp.einsum('cnab,bv->cnav', images, sin_space, precision=highest)
    spec_real = (jnp.einsum('ua,cnav->cnuv', cos_space, row_real, precision=highest) + jnp.einsum('ua,cnav->cnuv', sin_space, row_imag, precision=highest)) * factor
    spec_imag = (jnp.einsum('ua,cnav->cnuv', cos_space, row_imag, precision=highest) - jnp.einsum('ua,cnav->cnuv', sin_space, row_real, precision=highest)) * factor
    return (spec_real, spec_imag)

def inverse_spatial(spec_real, spec_imag, cos_space, sin_space):
    highest = lax.Precision.HIGHEST
    factor = 1.0 / cos_space.shape[0]
    col_real = jnp.einsum('au,cnuv->cnav', cos_space, spec_real, precision=highest) - jnp.einsum('au,cnuv->cnav', sin_space, spec_imag, precision=highest)
    col_imag = jnp.einsum('au,cnuv->cnav', cos_space, spec_imag, precision=highest) + jnp.einsum('au,cnuv->cnav', sin_space, spec_real, precision=highest)
    return (jnp.einsum('cnav,vb->cnab', col_real, cos_space, precision=highest) - jnp.einsum('cnav,vb->cnab', col_imag, sin_space, precision=highest)) * factor

def join(spec_real, spec_imag, gains, count):
    numerator_real = jnp.zeros(spec_real.shape[:1] + (count,) + spec_real.shape[2:], jnp.float32)
    numerator_imag = jnp.zeros_like(numerator_real)
    denominator = jnp.zeros(gains.shape[:1] + (count,) + gains.shape[2:], jnp.float32)
    for offset in range(5):
        gain = lax.slice_in_dim(gains, offset, offset + count, axis=1)
        numerator_real = numerator_real + gain * lax.slice_in_dim(spec_real, offset, offset + count, axis=1)
        numerator_imag = numerator_imag + gain * lax.slice_in_dim(spec_imag, offset, offset + count, axis=1)
        denominator = denominator + gain * gain
    denominator = denominator + noise_level
    return (numerator_real / denominator, numerator_imag / denominator)

def temporal(stacked, cutoff_local, channels):
    highest = lax.Precision.HIGHEST
    time_len = stacked.shape[1]
    cos_time, sin_time = tables(time_len)
    factor = 1.0 / math.sqrt(time_len)
    real = stacked[:channels]
    imag = stacked[channels:]
    freq_real = (jnp.einsum('wt,stk->swk', cos_time, real, precision=highest) + jnp.einsum('wt,stk->swk', sin_time, imag, precision=highest)) * factor
    freq_imag = (jnp.einsum('wt,stk->swk', cos_time, imag, precision=highest) - jnp.einsum('wt,stk->swk', sin_time, real, precision=highest)) * factor
    omega = jnp.arange(time_len, dtype=jnp.int32)
    distance = jnp.minimum(omega, time_len - omega)
    keeper = (distance[:, None] <= cutoff_local[None, :])[None]
    freq_real = jnp.where(keeper, freq_real, 0.0)
    freq_imag = jnp.where(keeper, freq_imag, 0.0)
    back_real = (jnp.einsum('tw,swk->stk', cos_time, freq_real, precision=highest) - jnp.einsum('tw,swk->stk', sin_time, freq_imag, precision=highest)) * factor
    back_imag = (jnp.einsum('tw,swk->stk', cos_time, freq_imag, precision=highest) + jnp.einsum('tw,swk->stk', sin_time, freq_real, precision=highest)) * factor
    return jnp.concatenate([back_real, back_imag], axis=0)

def reference(frames, transfer, cutoff):
    tiles_down = NY // SUBF
    tiles_across = NX // SUBF
    channels = tiles_down * tiles_across
    cos_space, sin_space = tables(SUBF)
    images = frames.astype(jnp.float32).reshape(TIME, tiles_down, SUBF, tiles_across, SUBF)
    images = images.transpose(1, 3, 0, 2, 4).reshape(channels, TIME, SUBF, SUBF)
    spec_real, spec_imag = forward_spatial(images, cos_space, sin_space)
    gains = transfer.astype(jnp.float32)[None]
    padding = ((0, 0), (2, 2), (0, 0), (0, 0))
    joined_real, joined_imag = join(jnp.pad(spec_real, padding), jnp.pad(spec_imag, padding), jnp.pad(gains, padding), TIME)
    stacked = jnp.concatenate([joined_real, joined_imag], axis=0).reshape(2 * channels, TIME, SUBF * SUBF)
    filtered = temporal(stacked, cutoff.reshape(-1), channels).reshape(2 * channels, TIME, SUBF, SUBF)
    result = inverse_spatial(filtered[:channels], filtered[channels:], cos_space, sin_space)
    result = result.reshape(tiles_down, tiles_across, TIME, SUBF, SUBF).transpose(2, 0, 3, 1, 4)
    return result.reshape(TIME, NY, NX)
```

```python
import functools
import math

import jax
import jax.numpy as jnp
import ml_dtypes
import numpy as np
from jax import lax
from jax.experimental import pallas as pl
from jax.experimental.pallas import tpu as pltpu
from jax.sharding import PartitionSpec as P

noise_level = 0.05
f32 = jnp.float32
bf16 = jnp.bfloat16
i16 = jnp.int16
TOP = 32766.0
STEPS = 256.0
TINY = 1e-30
VMEM_BYTES = 56 * 1024 * 1024


def real_basis(length, cosines_first):
    half = length // 2
    place = np.arange(length, dtype=np.int64)
    wave = np.arange(half + 1, dtype=np.int64)
    angles = (wave[:, None] * place[None, :] % length) * (2.0 * np.pi / length)
    cosines = np.cos(angles) * math.sqrt(2.0 / length)
    cosines[0] /= math.sqrt(2.0)
    cosines[half] /= math.sqrt(2.0)
    sines = np.sin(angles[1:half]) * math.sqrt(2.0 / length)
    return np.concatenate([cosines, sines], axis=0)


def split_table(table):
    high = table.astype(np.float32).astype(ml_dtypes.bfloat16)
    low = (table - high.astype(np.float64)).astype(np.float32).astype(ml_dtypes.bfloat16)
    return high, low


def left_split(table):
    high, low = split_table(table)
    return np.block([[high, high], [low, np.zeros_like(low)]])


def right_split(table):
    high, low = split_table(table)
    return np.block([[high, low], [high, np.zeros_like(low)]])


def band(length, reach):
    place = np.arange(length)
    near = (np.abs(place[:, None] - place[None, :]) <= reach).astype(np.float32)
    near = near.astype(ml_dtypes.bfloat16)
    return np.concatenate([near, near], axis=1)


def lane_choices(side):
    half = side // 2
    picks = np.zeros((side, 2 * side), np.float32)
    for lane in range(side):
        wave = half if lane == half else lane % half
        picks[wave, lane] = 1.0
        picks[wave if wave in (0, half) else side - wave, side + lane] = 1.0
    return picks.astype(ml_dtypes.bfloat16)


def dot(a, b):
    return jnp.dot(a, b, preferred_element_type=f32)


def pieces(x, axis):
    high = x.astype(bf16)
    low = (x - high.astype(f32)).astype(bf16)
    return jnp.concatenate([high, low], axis=axis)


def halves_sum(x, axis):
    size = x.shape[axis] // 2
    if axis == 0:
        return x[:size] + x[size:]
    return x[:, :size] + x[:, size:]


def special_lanes(shape, side):
    lane = lax.broadcasted_iota(jnp.int32, shape, len(shape) - 1) % side
    return (lane == 0) | (lane == side // 2)


def lane_signs(shape, side):
    lane = lax.broadcasted_iota(jnp.int32, shape, len(shape) - 1) % side
    return jnp.where(lane < side // 2, -1.0, 1.0).astype(f32)


def code_of(top):
    return jnp.ceil(jnp.log2(jnp.maximum(top, TINY)) * STEPS)


def prep_kernel(n, transfer_ref, *refs):
    outs, held = refs[:n], refs[n]
    count, side, _ = transfer_ref.shape
    half = side // 2
    groups = half // n
    me, core = lax.axis_index("tm"), lax.axis_index("cols")

    def fill(t, carry):
        held[pl.ds(pl.multiple_of(t * side, side), side), :] = transfer_ref[t].astype(f32)
        return carry

    lax.fori_loop(0, count, fill, 0)
    for shift in range(n):
        dest = lax.rem(me + shift, n)
        for j in range(groups):
            g = dest * groups + j
            minus = jnp.where(g == 0, half, side - g)
            row = jnp.where(core == 0, g, minus)
            outs[shift][j] = held[pl.ds(row, count, stride=side), :].astype(bf16)


def weight_kernel(n, cutoff_ref, picks_ref, band_ref, *refs):
    mine, theirs = refs[:n], refs[n : 2 * n]
    weight_ref, inverse_ref, kept_ref, rows, cuts = refs[2 * n :]
    groups, count, side = mine[0].shape
    half = side // 2
    time_len = n * count
    me, core = lax.axis_index("tm"), lax.axis_index("cols")
    for shift in range(n):
        source = lax.rem(me + n - shift, n)
        at = pl.ds(pl.multiple_of(source * count, count), count)
        for j in range(groups):
            rows[core, j, at, :] = mine[shift][j]
            rows[1 - core, j, at, :] = theirs[shift][j]
    picks = picks_ref[...]
    flipped = jnp.concatenate([picks[:, side:], picks[:, :side]], axis=1)
    for j in range(groups):
        g = me * groups + j
        cuts[0, pl.ds(j, 1), :] = cutoff_ref[pl.ds(g, 1), :].astype(f32)
        cuts[1, pl.ds(j, 1), :] = cutoff_ref[
            pl.ds(jnp.where(g == 0, half, side - g), 1), :
        ].astype(f32)

    def arrange(plus, minus, first):
        a, c = plus[:, :side], plus[:, side:]
        b, d = minus[:, :side], minus[:, side:]
        early = jnp.concatenate([a, jnp.where(first, d, c)], axis=1)
        late = jnp.concatenate([jnp.where(first, c, b), jnp.where(first, b, d)], axis=1)
        return early, late

    cut_plus = dot(cuts[0].astype(bf16), picks)
    cut_minus = dot(cuts[1].astype(bf16), flipped)
    row = lax.broadcasted_iota(jnp.int32, (groups, side), 0)
    early, late = arrange(cut_plus, cut_minus, (row == 0) & (me == 0))
    kept_ref[0] = early
    kept_ref[1] = late

    def one(j, carry):
        plus = dot(rows[0, j], picks)
        minus = dot(rows[1, j], flipped)
        first = jnp.full((time_len, side), me * groups + j) == 0
        for order, weight in enumerate(arrange(plus, minus, first)):
            weight_ref[j, order] = weight.astype(bf16)
            total = dot(band_ref[...], pieces(weight * weight, 0))
            inverse_ref[j, order] = 1.0 / (total + noise_level)
        return carry

    lax.fori_loop(0, groups, one, 0)


def quantize_rows(values_ref, tops_ref, out_ref, series, count, side):
    codes = code_of(tops_ref[...])
    out_ref[series * count :, :] = codes.astype(jnp.int32).astype(i16)
    tops_ref[...] = jnp.exp2(codes * (-1.0 / STEPS)) * TOP

    def one(j, carry):
        scaled = values_ref[j] * tops_ref[pl.ds(j, 1), :]
        at = pl.ds(pl.multiple_of(j * count, count), count)
        out_ref[at, :] = jnp.round(scaled).astype(jnp.int32).astype(i16)
        return carry

    lax.fori_loop(0, series, one, 0, unroll=4)


def scales_of(in_ref, series, count):
    codes = in_ref[series * count :, :].astype(jnp.int32).astype(f32)
    return jnp.exp2(codes * (1.0 / STEPS)) * (1.0 / TOP)


def forward_kernel(n, frames_ref, left_ref, right_ref, *refs):
    outs, spectra, values, tops = refs[:n], *refs[n:]
    count, side, _ = frames_ref.shape
    half = side // 2
    groups = half // n
    series = 2 * groups
    me = lax.axis_index("tm")

    def transform(pair, carry):
        t = pair * 2
        both = jnp.concatenate([frames_ref[t], frames_ref[t + 1]], axis=1)
        rows = halves_sum(dot(left_ref[...], both), 0)
        for k in range(2):
            split = pieces(rows[:, k * side : (k + 1) * side], 1)
            at = pl.ds(pl.multiple_of((t + k) * side, side), side)
            spectra[at, :] = halves_sum(dot(split, right_ref[...]), 1)
        return carry

    lax.fori_loop(0, count // 2, transform, 0, unroll=2)
    single = special_lanes((count, side), side)
    signs = lane_signs((count, side), side)
    for shift in range(n):
        dest = lax.rem(me + shift, n)

        def butterfly(j, carry):
            g = dest * groups + j
            even = spectra[pl.ds(g, count, stride=side), :]
            odd = spectra[pl.ds(half + g, count, stride=side), :]
            mixed = pltpu.roll(odd, half, 1) * signs
            alone = single | (jnp.full((count, side), g) == 0)
            first = even + jnp.where(alone, 0.0, mixed)
            second = jnp.where(alone, odd, even - mixed)
            values[j] = first
            values[groups + j] = second
            tops[pl.ds(j, 1), :] = jnp.max(jnp.abs(first), axis=0, keepdims=True)
            tops[pl.ds(groups + j, 1), :] = jnp.max(jnp.abs(second), axis=0, keepdims=True)
            return carry

        lax.fori_loop(0, groups, butterfly, 0, unroll=2)
        quantize_rows(values, tops, outs[shift], series, count, side)


def filter_kernel(n, weight_ref, inverse_ref, kept_ref, band_ref, time_ref, back_ref, *refs):
    ins, outs = refs[:n], refs[n : 2 * n]
    scales, joined, values, tops = refs[2 * n :]
    groups, _, time_len, wide = weight_ref.shape
    side = wide // 2
    count = time_len // n
    series = 2 * groups
    me = lax.axis_index("tm")
    for shift in range(n):
        scales[shift] = scales_of(ins[shift], series, count)
    row = lax.broadcasted_iota(jnp.int32, (time_len, wide), 0)
    distance = jnp.where(row <= time_len // 2, row, row - time_len // 2).astype(f32)

    def one(j, carry):
        for shift in range(n):
            source = lax.rem(me + n - shift, n)
            at = pl.ds(pl.multiple_of(source * count, count), count)
            for k in range(2):
                s = k * groups + j
                part = ins[shift][pl.ds(pl.multiple_of(s * count, count), count), :]
                part = part.astype(jnp.int32).astype(f32) * scales[shift, pl.ds(s, 1), :]
                joined[at, k * side : (k + 1) * side] = part
        spectra = joined[...]
        total = None
        for order in range(2):
            terms = weight_ref[j, order].astype(f32) * spectra
            ratio = dot(band_ref[...], pieces(terms, 0)) * inverse_ref[j, order]
            coefficients = halves_sum(dot(time_ref[...], pieces(ratio, 0)), 0)
            keep = distance <= kept_ref[order, pl.ds(j, 1), :]
            coefficients = jnp.where(keep, coefficients, 0.0)
            total = coefficients if total is None else total + coefficients
        back = halves_sum(dot(back_ref[...], pieces(total, 0)), 0)
        joined[...] = back
        for shift in range(n):
            dest = lax.rem(me + shift, n)
            at = pl.ds(pl.multiple_of(dest * count, count), count)
            for k in range(2):
                s = k * groups + j
                part = joined[at, k * side : (k + 1) * side]
                values[shift, s] = part
                tops[shift, pl.ds(s, 1), :] = jnp.max(jnp.abs(part), axis=0, keepdims=True)
        return carry

    lax.fori_loop(0, groups, one, 0)
    for shift in range(n):
        quantize_rows(values.at[shift], tops.at[shift], outs[shift], series, count, side)


def inverse_kernel(n, aliased, left_ref, right_ref, *refs):
    ins, refs = refs[:n], refs[n:]
    if aliased:
        refs = refs[1:]
    out_ref, scales, packed, rows = refs
    count, side, _ = out_ref.shape
    half = side // 2
    groups = half // n
    series = 2 * groups
    me = lax.axis_index("tm")
    single = special_lanes((count, side), side)
    signs = -lane_signs((count, side), side)
    for shift in range(n):
        dest = lax.rem(me + n - shift, n)
        scales[...] = scales_of(ins[shift], series, count)

        def butterfly(j, carry):
            g = dest * groups + j
            parts = []
            for k in range(2):
                s = k * groups + j
                part = ins[shift][pl.ds(pl.multiple_of(s * count, count), count), :]
                parts.append(part.astype(jnp.int32).astype(f32) * scales[pl.ds(s, 1), :])
            first, second = parts
            alone = single | (jnp.full((count, side), g) == 0)
            mixed = pltpu.roll((first - second) * 0.5, half, 1) * signs
            even = jnp.where(alone, first, (first + second) * 0.5)
            odd = jnp.where(alone, second, mixed)
            packed[pl.ds(pl.multiple_of(j * count, count), count), :] = pieces(even, 1)
            packed[pl.ds(pl.multiple_of((groups + j) * count, count), count), :] = pieces(odd, 1)
            return carry

        lax.fori_loop(0, groups, butterfly, 0, unroll=2)
        for k in range(2):
            size = groups * count
            done = halves_sum(dot(packed[k * size : (k + 1) * size, :], right_ref[...]), 1)
            start = (k * half + dest * groups) * count
            rows[pl.ds(pl.multiple_of(start, size), size), :] = done

    def transform(pair, carry):
        t = pair * 2
        both = jnp.concatenate(
            [
                rows[pl.ds(t, side, stride=count), :],
                rows[pl.ds(t + 1, side, stride=count), :],
            ],
            axis=1,
        )
        done = halves_sum(dot(left_ref[...], pieces(both, 0)), 0)
        out_ref[t] = done[:, :side]
        out_ref[t + 1] = done[:, side:]
        return carry

    lax.fori_loop(0, count // 2, transform, 0, unroll=2)


def params():
    return pltpu.CompilerParams(vmem_limit_bytes=VMEM_BYTES)


def cost(flops, size):
    return pl.CostEstimate(flops=int(flops), bytes_accessed=int(size), transcendentals=0)


def shifted(block, axis, n, shift):
    if shift == 0:
        return block
    return lax.ppermute(block, axis, [(k, (k + shift) % n) for k in range(n)])


def on_device_fast(n, frames, transfer, cutoff):
    count, side = frames.shape[0], transfer.shape[1]
    across = frames.shape[2] // side
    half = side // 2
    groups = half // n
    series = 2 * groups
    time_len = n * count
    space = real_basis(side, False)
    clock = real_basis(time_len, True)
    spatial_left = jnp.asarray(np.concatenate(split_table(space), axis=0))
    spatial_right = jnp.asarray(right_split(space.T))
    inverse_left = jnp.asarray(left_split(space.T))
    inverse_right = jnp.asarray(right_split(space))
    time_left = jnp.asarray(left_split(clock))
    back_left = jnp.asarray(left_split(0.5 * clock.T))
    banded = jnp.asarray(band(time_len, 2))
    picks = jnp.asarray(lane_choices(side))
    block = jax.ShapeDtypeStruct((series * count + series, side), i16)
    sds = jax.ShapeDtypeStruct

    shares = pl.pallas_call(
        functools.partial(prep_kernel, n),
        out_shape=[sds((groups, count, side), bf16)] * n,
        scratch_shapes=[pltpu.VMEM((count * side, side), f32)],
        compiler_params=params(),
        cost_estimate=cost(0, 4 * transfer.size),
        name="prep",
    )(transfer)
    mine = [shifted(shares[s], "tm", n, s) for s in range(n)]
    theirs = [lax.ppermute(share, "cols", [(0, 1), (1, 0)]) for share in mine]

    received = []
    for channel in range(across):
        blocks = pl.pallas_call(
            functools.partial(forward_kernel, n),
            out_shape=[block] * n,
            grid=(1,),
            in_specs=[
                pl.BlockSpec((count, side, side), lambda _, c=channel: (0, 0, c)),
                pl.BlockSpec(spatial_left.shape, lambda _: (0, 0)),
                pl.BlockSpec(spatial_right.shape, lambda _: (0, 0)),
            ],
            out_specs=[pl.BlockSpec(block.shape, lambda _: (0, 0))] * n,
            scratch_shapes=[
                pltpu.VMEM((count * side, side), f32),
                pltpu.VMEM((series, count, side), f32),
                pltpu.VMEM((series, side), f32),
            ],
            compiler_params=params(),
            cost_estimate=cost(count * side**3 * 12, count * side * side * 8),
            name="forward",
        )(frames, spatial_left, spatial_right)
        received.append([shifted(blocks[s], "tm", n, s) for s in range(n)])

    weight, inverse, kept = pl.pallas_call(
        functools.partial(weight_kernel, n),
        out_shape=[
            sds((groups, 2, time_len, 2 * side), bf16),
            sds((groups, 2, time_len, 2 * side), f32),
            sds((2, groups, 2 * side), f32),
        ],
        scratch_shapes=[
            pltpu.VMEM((2, groups, time_len, side), bf16),
            pltpu.VMEM((2, groups, side), f32),
        ],
        compiler_params=params(),
        cost_estimate=cost(groups * time_len * side * side * 24, groups * time_len * side * 28),
        name="weights",
    )(cutoff, picks, banded, *mine, *theirs)

    returned = []
    for channel in range(across):
        blocks = pl.pallas_call(
            functools.partial(filter_kernel, n),
            out_shape=[block] * n,
            scratch_shapes=[
                pltpu.VMEM((n, series, side), f32),
                pltpu.VMEM((time_len, 2 * side), f32),
                pltpu.VMEM((n, series, count, side), f32),
                pltpu.VMEM((n, series, side), f32),
            ],
            compiler_params=params(),
            cost_estimate=cost(groups * time_len**2 * side * 80, groups * time_len * side * 40),
            name="filter",
        )(weight, inverse, kept, banded, time_left, back_left, *received[channel])
        returned.append([shifted(blocks[s], "tm", n, s) for s in range(n)])

    restored = None
    for channel in range(across):
        aliased = restored is not None
        operands = [inverse_left, inverse_right, *returned[channel]]
        in_specs = [
            pl.BlockSpec(inverse_left.shape, lambda _: (0, 0)),
            pl.BlockSpec(inverse_right.shape, lambda _: (0, 0)),
        ] + [pl.BlockSpec(block.shape, lambda _: (0, 0))] * n
        if aliased:
            operands.append(restored)
            in_specs.append(pl.BlockSpec(memory_space=pl.ANY))
        restored = pl.pallas_call(
            functools.partial(inverse_kernel, n, aliased),
            out_shape=sds((count, side, across * side), f32),
            grid=(1,),
            in_specs=in_specs,
            out_specs=pl.BlockSpec((count, side, side), lambda _, c=channel: (0, 0, c)),
            scratch_shapes=[
                pltpu.VMEM((series, side), f32),
                pltpu.VMEM((series * count, 2 * side), bf16),
                pltpu.VMEM((side * count, side), f32),
            ],
            input_output_aliases={len(operands) - 1: 0} if aliased else {},
            compiler_params=params(),
            cost_estimate=cost(count * side**3 * 14, count * side * side * 8),
            name="inverse",
        )(*operands)
    return restored


def with_halo(cells, sides, width):
    for axis, dim in sides:
        count = lax.axis_size(axis)
        ends = count - 1
        head = lax.slice_in_dim(cells, 0, width, axis=dim)
        tail = lax.slice_in_dim(cells, cells.shape[dim] - width, cells.shape[dim], axis=dim)
        cells = jnp.concatenate(
            [
                lax.ppermute(tail, axis, [(i, (i + 1) % count) for i in range(ends)]),
                cells,
                lax.ppermute(head, axis, [((i + 1) % count, i) for i in range(ends)]),
            ],
            axis=dim,
        )
    return cells


def tables(length):
    series = jnp.arange(length, dtype=jnp.int32)
    product = series[:, None] * series[None, :] % length
    angles = product.astype(jnp.float32) * (2.0 * math.pi / length)
    return (jnp.cos(angles), jnp.sin(angles))


def forward_spatial(images, cos_space, sin_space):
    highest = lax.Precision.HIGHEST
    factor = 1.0 / cos_space.shape[0]
    row_real = jnp.einsum("cnab,bv->cnav", images, cos_space, precision=highest)
    row_imag = -jnp.einsum("cnab,bv->cnav", images, sin_space, precision=highest)
    spec_real = (
        jnp.einsum("ua,cnav->cnuv", cos_space, row_real, precision=highest)
        + jnp.einsum("ua,cnav->cnuv", sin_space, row_imag, precision=highest)
    ) * factor
    spec_imag = (
        jnp.einsum("ua,cnav->cnuv", cos_space, row_imag, precision=highest)
        - jnp.einsum("ua,cnav->cnuv", sin_space, row_real, precision=highest)
    ) * factor
    return (spec_real, spec_imag)


def inverse_spatial(spec_real, spec_imag, cos_space, sin_space):
    highest = lax.Precision.HIGHEST
    factor = 1.0 / cos_space.shape[0]
    col_real = jnp.einsum("au,cnuv->cnav", cos_space, spec_real, precision=highest) - jnp.einsum(
        "au,cnuv->cnav", sin_space, spec_imag, precision=highest
    )
    col_imag = jnp.einsum("au,cnuv->cnav", cos_space, spec_imag, precision=highest) + jnp.einsum(
        "au,cnuv->cnav", sin_space, spec_real, precision=highest
    )
    return (
        jnp.einsum("cnav,vb->cnab", col_real, cos_space, precision=highest)
        - jnp.einsum("cnav,vb->cnab", col_imag, sin_space, precision=highest)
    ) * factor


def join(spec_real, spec_imag, gains, count):
    numerator_real = jnp.zeros(spec_real.shape[:1] + (count,) + spec_real.shape[2:], jnp.float32)
    numerator_imag = jnp.zeros_like(numerator_real)
    denominator = jnp.zeros(gains.shape[:1] + (count,) + gains.shape[2:], jnp.float32)
    for offset in range(5):
        gain = lax.slice_in_dim(gains, offset, offset + count, axis=1)
        numerator_real = numerator_real + gain * lax.slice_in_dim(
            spec_real, offset, offset + count, axis=1
        )
        numerator_imag = numerator_imag + gain * lax.slice_in_dim(
            spec_imag, offset, offset + count, axis=1
        )
        denominator = denominator + gain * gain
    denominator = denominator + noise_level
    return (numerator_real / denominator, numerator_imag / denominator)


def temporal(stacked, cutoff_local, channels):
    highest = lax.Precision.HIGHEST
    time_len = stacked.shape[1]
    cos_time, sin_time = tables(time_len)
    factor = 1.0 / math.sqrt(time_len)
    real = stacked[:channels]
    imag = stacked[channels:]
    freq_real = (
        jnp.einsum("wt,stk->swk", cos_time, real, precision=highest)
        + jnp.einsum("wt,stk->swk", sin_time, imag, precision=highest)
    ) * factor
    freq_imag = (
        jnp.einsum("wt,stk->swk", cos_time, imag, precision=highest)
        - jnp.einsum("wt,stk->swk", sin_time, real, precision=highest)
    ) * factor
    omega = jnp.arange(time_len, dtype=jnp.int32)
    distance = jnp.minimum(omega, time_len - omega)
    keeper = (distance[:, None] <= cutoff_local[None, :])[None]
    freq_real = jnp.where(keeper, freq_real, 0.0)
    freq_imag = jnp.where(keeper, freq_imag, 0.0)
    back_real = (
        jnp.einsum("tw,swk->stk", cos_time, freq_real, precision=highest)
        - jnp.einsum("tw,swk->stk", sin_time, freq_imag, precision=highest)
    ) * factor
    back_imag = (
        jnp.einsum("tw,swk->stk", cos_time, freq_imag, precision=highest)
        + jnp.einsum("tw,swk->stk", sin_time, freq_real, precision=highest)
    ) * factor
    return jnp.concatenate([back_real, back_imag], axis=0)


def to_channels(images, side, across):
    total = images.shape[0]
    return images.reshape(total, side, across, side).transpose(2, 0, 1, 3)


def on_device_plain(frames, transfer, cutoff):
    count = frames.shape[0]
    side = transfer.shape[1]
    across = frames.shape[2] // side
    cos_space, sin_space = tables(side)
    packed = jnp.concatenate([frames, transfer], axis=2)
    extended = with_halo(packed, (("tm", 0),), 2)
    images = to_channels(extended[:, :, : across * side].astype(jnp.float32), side, across)
    spec_real, spec_imag = forward_spatial(images, cos_space, sin_space)
    gains = extended[:, :, across * side :].astype(jnp.float32)[None]
    joined_real, joined_imag = join(spec_real, spec_imag, gains, count)
    payload = jnp.concatenate([joined_real, joined_imag], axis=0).reshape(
        2 * across, count, side * side
    )
    gathered = lax.all_to_all(payload, "tm", split_axis=2, concat_axis=1, tiled=True)
    width = gathered.shape[2]
    start = lax.axis_index("tm") * width
    cutoff_local = lax.dynamic_slice_in_dim(cutoff.reshape(-1), start, width)
    filtered = temporal(gathered, cutoff_local, across)
    returned = lax.all_to_all(filtered, "tm", split_axis=1, concat_axis=2, tiled=True)
    spectra_back = returned.reshape(2 * across, count, side, side)
    result = inverse_spatial(spectra_back[:across], spectra_back[across:], cos_space, sin_space)
    return result.transpose(1, 2, 0, 3).reshape(count, side, across * side)


def on_device(frames, transfer, cutoff):
    n = lax.axis_size("tm")
    count, side = frames.shape[0], transfer.shape[1]
    tiled = side == 128 and frames.shape[1] == side and count % 32 == 0 and (n * count) % 128 == 0
    if tiled and lax.axis_size("cols") == 2 and (side // 2) % n == 0 and side // n % 32 == 0:
        return on_device_fast(n, frames, transfer, cutoff)
    return on_device_plain(frames, transfer, cutoff)


def solution(mesh):
    return jax.shard_map(
        on_device,
        mesh=mesh,
        in_specs=(P(("parts", "tm"), "rows", "cols"), P(("parts", "tm"), None, None), P()),
        out_specs=P(("parts", "tm"), "rows", "cols"),
        check_vma=False,
    )
```
